32 devices in a mesh: blk: 16 (over z, y, x), feat: 2 (over core).
Axes of the slice: x: 2, y: 2, z: 4, core: 2. Of those that a mesh axis runs over, the one named last changes fastest.
Arguments:
- points: bfloat16 [16384, 64], P('blk', 'feat'), may hold values from -1.5 to 1.5
- vectors: bfloat16 [16384, 64], P('blk', 'feat'), may hold values from -5.5 to 5.5
- lengthscale: float32 [64], replicated, may hold values from 0.5 to 2
- outscale: float32 [1], replicated, may hold values from 0.1 to 0.4
- noise: float32 [1], replicated, may hold values from 0.05 to 0.5
Outputs:
- product: float32 [16384, 64], P('blk', 'feat')
The draws below stay inside these ranges and needn't reach their ends.
All inputs are finite; a program needn't handle non-finite values.
Results may differ from the reference program's by a relative error of at most 0.0026.
Values may be sent and summed in bfloat16 or wider, within the bound.
A program may use at most 64 MiB of HBM per device.

```python
import math
import jax
import jax.numpy as jnp
from jax import lax

FEATS = 64
VECS = 64
PTS_DEV = 1024
POINTS = 16384


def draw_points(key, part):
    latent_width = FEATS // 4
    key_latent, key_map, key_noise, key_level = jax.random.split(jax.random.fold_in(key, 7), 4)
    spread = (0.5 / (FEATS * 1.35)) ** 0.5
    mapping = jax.random.normal(key_map, (latent_width, FEATS), jnp.float32) * spread
    jitter_level = jnp.exp(jax.random.uniform(key_level, (POINTS, 1), jnp.float32, math.log(0.04), math.log(0.3)))
    latent = jax.random.normal(key_latent, (POINTS, latent_width), jnp.float32)
    jitter = jax.random.normal(key_noise, (POINTS, FEATS), jnp.float32) * jitter_level
    values = jnp.dot(latent, mapping) + jitter
    return jnp.clip(values, -1.5, 1.5).astype(jnp.bfloat16)


def draw_vectors(key, part):
    key_noise, key_sign, key_size = jax.random.split(jax.random.fold_in(key, 11), 3)
    signs = jnp.where(jax.random.bernoulli(key_sign, 0.5, (VECS,)), 1.0, -1.0).astype(jnp.float32)
    offsets = signs * jax.random.uniform(key_size, (VECS,), jnp.float32, 0.75, 1.5)
    spread_part = jnp.clip(jax.random.normal(key_noise, (POINTS, VECS), jnp.float32), -4.0, 4.0)
    return (spread_part + offsets[None, :]).astype(jnp.bfloat16)


def setup_inputs(seed: int = 0) -> dict:
    key_of = jax.random.split(jax.random.key(seed), 6)
    return {
        "points": draw_points(jax.random.fold_in(key_of[5], 71), 0),
        "vectors": draw_vectors(jax.random.fold_in(key_of[5], 71), 0),
        "lengthscale": jnp.clip(jnp.exp(jax.random.uniform(key_of[2], (FEATS,), jnp.float32, math.log(0.5), math.log(2.0))), 0.5, 2.0),
        "outscale": jnp.clip(jnp.exp(jax.random.uniform(key_of[3], (1,), jnp.float32, math.log(0.1), math.log(0.4))), 0.1, 0.4),
        "noise": jnp.clip(jnp.exp(jax.random.uniform(key_of[4], (1,), jnp.float32, math.log(0.05), math.log(0.5))), 0.05, 0.5),
    }


def reference(points, vectors, lengthscale, outscale, noise):
    scaled = (points.astype(jnp.float32) / lengthscale).astype(jnp.bfloat16).astype(jnp.float32)
    norms = jnp.sum(scaled * scaled, axis=1)
    vector_wide = vectors.astype(jnp.float32)
    row_blocks = scaled.reshape(POINTS // PTS_DEV, PTS_DEV, FEATS)
    norm_blocks = norms.reshape(POINTS // PTS_DEV, PTS_DEV)

    def one_block(paired):
        block_rows, block_norms = paired
        inner = jnp.dot(block_rows, scaled.T, precision=lax.Precision.HIGHEST)
        distance = jnp.maximum(block_norms[:, None] + norms[None, :] - 2.0 * inner, 0.0)
        kernel_block = (outscale[0] * jnp.exp(-0.5 * distance)).astype(jnp.bfloat16).astype(jnp.float32)
        return jnp.dot(kernel_block, vector_wide, precision=lax.Precision.HIGHEST)

    result = lax.map(one_block, (row_blocks, norm_blocks)).reshape(POINTS, VECS)
    return result + noise[0] * vector_wide
```

```python
import functools

import jax
import jax.numpy as jnp
from jax import lax
from jax.experimental import pallas as pl
from jax.experimental.pallas import tpu as pltpu
from jax.sharding import PartitionSpec as P

LOG2E = 1.4426950408889634
F32 = jnp.float32
BF16 = jnp.bfloat16
EXTRA = 16


def pieces(value):
    first = value.astype(BF16).astype(F32)
    rest = value - first
    second = rest.astype(BF16).astype(F32)
    return first, second, rest - second


def extra_rows(rows):
    shape = (EXTRA, rows[0].shape[1])
    place = lax.broadcasted_iota(jnp.int32, shape, 0)
    out = jnp.zeros(shape, F32)
    for index, row in enumerate(rows):
        out = jnp.where(place == index, row, out)
    return out.astype(BF16)


def visit_order(line, inner):
    if inner == 1:
        return [(rank, 0, 0) for rank in range(line)]
    near = [(rank, b, 0) for rank in range(line) for b in range(2)]
    order = []
    sent = 0
    for place, item in enumerate(near):
        order.append(item)
        if place >= 2:
            order.append((near[sent][0], near[sent][1], 1))
            sent += 1
    order += [(near[i][0], near[i][1], 1) for i in range(sent, len(near))]
    return order


def pick(step, values):
    out = jnp.int32(values[0])
    for index, value in enumerate(values):
        if value != values[0]:
            out = jnp.where(step == index, jnp.int32(value), out)
    return out


def kernel(
    line, inner, points, vectors, lengths, outscale, noise, result,
    blocks, own, own_wide, total, inbox, mine,
    local_sem, pair_send, pair_recv, line_send, b_send, c_send, recv, part_send, part_recv,
):
    me = lax.axis_index("blk")
    core = lax.axis_index("feat")
    other = 1 - core
    half, rows = points.shape
    feats = own.shape[0]
    share = rows // 2
    z = me // (inner * inner)
    stride_b = jnp.where(core == 0, inner, 1)
    stride_c = jnp.where(core == 0, 1, inner)
    low = me % inner
    high = (me // inner) % inner
    bit_b = jnp.where(core == 0, high, low)
    bit_c = jnp.where(core == 0, low, high)
    peer_b = me + stride_b * (1 - 2 * bit_b)
    peer_c = me + stride_c * (1 - 2 * bit_c)
    step_z = inner * inner
    has_up = z < line - 1
    has_down = z > 0

    def place_of(blk, feat):
        return {"blk": blk, "feat": feat}

    def remote(src, dst, send, arrive, blk, feat):
        return pltpu.make_async_remote_copy(
            src_ref=src, dst_ref=dst, send_sem=send, recv_sem=arrive,
            device_id=place_of(blk, feat), device_id_type=pl.DeviceIdType.MESH,
        )

    barrier = pltpu.get_barrier_semaphore()

    def greet(blk, feat):
        pl.semaphore_signal(
            barrier, inc=1, device_id=place_of(blk, feat), device_id_type=pl.DeviceIdType.MESH
        )

    greet(me, other)
    if inner == 2:
        greet(peer_b, core)
        greet(peer_c, core)

    @pl.when(has_up)
    def _():
        greet(me + step_z, core)

    @pl.when(has_down)
    def _():
        greet(me - step_z, core)

    mine_cols = pl.ds(pl.multiple_of(core * share, share), share)
    their_cols = pl.ds(pl.multiple_of(other * share, share), share)
    my_rows = pl.ds(pl.multiple_of(core * half, half), half)
    my_vector_rows = pl.ds(pl.multiple_of(feats + core * half, half), half)
    locals_ = [
        pltpu.make_async_copy(
            points.at[:, mine_cols], blocks.at[me, my_rows, :], local_sem.at[0]),
        pltpu.make_async_copy(
            vectors.at[:, mine_cols], blocks.at[me, my_vector_rows, :], local_sem.at[1]),
        pltpu.make_async_copy(points, own.at[my_rows, :], local_sem.at[2]),
        pltpu.make_async_copy(vectors, mine, local_sem.at[3]),
    ]
    for copy in locals_:
        copy.start()

    neighbours = (1 + 2 * (inner - 1)) + has_up.astype(jnp.int32) + has_down.astype(jnp.int32)
    pl.semaphore_wait(barrier, neighbours)

    pair = [
        remote(points.at[:, their_cols], blocks.at[me, my_rows, :],
               pair_send.at[0], pair_recv.at[0], me, other),
        remote(vectors.at[:, their_cols], blocks.at[me, my_vector_rows, :],
               pair_send.at[1], pair_recv.at[1], me, other),
        remote(points, own.at[my_rows, :], pair_send.at[2], pair_recv.at[2], me, other),
    ]
    for copy in pair:
        copy.start()

    def line_copy(block, direction, zz):
        target = jnp.where(direction == 0, me + step_z, me - step_z)
        return remote(blocks.at[block], blocks.at[block], line_send.at[direction, zz],
                      recv.at[block], target, core)

    def b_copy(block, zz):
        return remote(blocks.at[block], blocks.at[block], b_send.at[zz],
                      recv.at[block], peer_b, core)

    def c_copy(block, slot):
        return remote(blocks.at[block], blocks.at[block], c_send.at[slot],
                      recv.at[block], peer_c, core)

    def line_id(zz, b, c):
        return zz * step_z + (bit_b ^ b) * stride_b + (bit_c ^ c) * stride_c

    order = visit_order(line, inner)
    middle = jnp.minimum(z, line - 1 - z)
    more_up = z < line - 1 - z

    def locate(step):
        rank = pick(step, [item[0] for item in order])
        b = pick(step, [item[1] for item in order])
        c = pick(step, [item[2] for item in order])
        both = rank <= 2 * middle
        distance = jnp.where(both, (rank + 1) // 2, rank - middle)
        upward = jnp.where(both, rank % 2 == 1, more_up)
        zz = jnp.where(upward, z + distance, z - distance)
        return zz, b, c, line_id(zz, b, c)

    def forward(zz, b, c, block):
        @pl.when((b == 0) & (c == 0) & (zz <= z) & has_up)
        def _():
            line_copy(block, 0, zz).start()

        @pl.when((b == 0) & (c == 0) & (zz >= z) & has_down)
        def _():
            line_copy(block, 1, zz).start()

        if inner == 2:
            @pl.when((b == 0) & (c == 0))
            def _():
                b_copy(block, zz).start()

            @pl.when(c == 0)
            def _():
                c_copy(block, zz * 2 + b).start()

    scale = outscale[0]
    top = jnp.log(jnp.full((1, 1), scale, F32)) * LOG2E
    column = jnp.transpose(jnp.broadcast_to(lengths[...], (feats, feats)))[:, 0:1]

    for copy in locals_[:2]:
        copy.wait()
    pair[0].wait_recv()
    pair[1].wait_recv()
    forward(z, jnp.int32(0), jnp.int32(0), me)

    locals_[2].wait()
    pair[2].wait_recv()
    scaled = (own[...].astype(F32) / column).astype(BF16).astype(F32)
    level = -0.5 * LOG2E * jnp.sum(scaled * scaled, axis=0, keepdims=True) + top
    ones = jnp.ones_like(level)
    for index, piece in enumerate(pieces(scaled * LOG2E)):
        own_wide[index * feats:(index + 1) * feats, :] = piece.astype(BF16)
    own_wide[3 * feats:, :] = extra_rows((ones, ones, ones) + pieces(level))
    total[...] = jnp.zeros_like(total)

    def visit(step, carry):
        zz, b, c, block = locate(step)

        @pl.when(step > 0)
        def _():
            c_copy(block, 0).wait_recv()
            forward(zz, b, c, block)

        guest = (blocks[block, 0:feats, :].astype(F32) / column).astype(BF16)
        wide = guest.astype(F32)
        norm = -0.5 * LOG2E * jnp.sum(wide * wide, axis=0, keepdims=True)
        one = jnp.ones_like(norm)
        right = jnp.concatenate(
            [guest, guest, guest, extra_rows(pieces(norm) + (one, one, one))], axis=0)
        power = jnp.dot(right.T, own_wide[...], preferred_element_type=F32)
        value = jnp.exp2(jnp.minimum(power, top)).astype(BF16)
        total[...] += jnp.dot(blocks[block, feats:, :], value, preferred_element_type=F32)
        return carry

    lax.fori_loop(0, len(order), visit, 0)

    other_rows = pl.ds(pl.multiple_of(other * half, half), half)
    part = remote(total.at[other_rows, :], inbox, part_send, part_recv, me, other)
    part.start()
    locals_[3].wait()
    part.wait_recv()
    result[...] = total[my_rows, :] + inbox[...] + noise[0] * mine[...].astype(F32)

    part.wait_send()
    for copy in pair:
        copy.wait_send()

    def drain(zz, carry):
        block = line_id(zz, 0, 0)

        @pl.when((zz <= z) & has_up)
        def _():
            line_copy(block, 0, zz).wait_send()

        @pl.when((zz >= z) & has_down)
        def _():
            line_copy(block, 1, zz).wait_send()

        if inner == 2:
            b_copy(block, zz).wait_send()
            c_copy(block, zz * 2).wait_send()
            c_copy(block, zz * 2 + 1).wait_send()
        return carry

    lax.fori_loop(0, line, drain, 0)


def per_device(blk, points, vectors, lengthscale, outscale, noise):
    inner = 2 if blk % 4 == 0 else 1
    line = blk // (inner * inner)
    rows, half = points.shape
    feats = 2 * half
    share = rows // 2
    vmem = pl.BlockSpec(memory_space=pltpu.VMEM)
    smem = pl.BlockSpec(memory_space=pltpu.SMEM)
    anywhere = pl.BlockSpec(memory_space=pl.ANY)
    dma = pltpu.SemaphoreType.DMA
    out = pl.pallas_call(
        functools.partial(kernel, line, inner),
        out_shape=jax.ShapeDtypeStruct((half, rows), F32),
        in_specs=[anywhere, anywhere, vmem, smem, smem],
        out_specs=vmem,
        scratch_shapes=[
            pltpu.VMEM((blk, 2 * feats, share), BF16),
            pltpu.VMEM((feats, rows), BF16),
            pltpu.VMEM((3 * feats + EXTRA, rows), BF16),
            pltpu.VMEM((feats, rows), F32),
            pltpu.VMEM((half, rows), F32),
            pltpu.VMEM((half, rows), BF16),
            dma((4,)),
            dma((3,)),
            dma((3,)),
            dma((2, line)),
            dma((line,)),
            dma((2 * line,)),
            dma((blk,)),
            dma,
            dma,
        ],
        compiler_params=pltpu.CompilerParams(
            collective_id=0, has_side_effects=True, vmem_limit_bytes=48 << 20
        ),
        name="gather_solve",
    )(points.T, vectors.T, lengthscale.reshape(1, feats), outscale, noise)
    return out.T


def solution(mesh):
    placed = (P("blk", "feat"), P("blk", "feat"), P(), P(), P())
    return jax.shard_map(
        functools.partial(per_device, mesh.shape["blk"]),
        mesh=mesh, in_specs=placed, out_specs=P("blk", "feat"), check_vma=False,
    )
```

```python
import functools

import jax
import jax.numpy as jnp
from jax import lax
from jax.experimental import pallas as pl
from jax.experimental.pallas import tpu as pltpu
from jax.sharding import PartitionSpec as P

LOG2E = 1.4426950408889634
F32 = jnp.float32
BF16 = jnp.bfloat16
EXTRA = 16
SIDE = 2
PLANE = SIDE * SIDE


def pieces(value):
    first = value.astype(BF16).astype(F32)
    rest = value - first
    second = rest.astype(BF16).astype(F32)
    return first, second, rest - second


def extra_rows(rows):
    shape = (EXTRA, rows[0].shape[1])
    place = lax.broadcasted_iota(jnp.int32, shape, 0)
    out = jnp.zeros(shape, F32)
    for index, row in enumerate(rows):
        out = jnp.where(place == index, row, out)
    return out.astype(BF16)


def kernel(
    line, points, vectors, lengths, outscale, noise, result,
    columns, row_points, right, left, total, inbox, mine, swap_out, swap_in,
    local_sem, pair_send, pair_recv, plane_send, plane_recv, twin_send, twin_recv,
    row_send, row_recv, part_send, part_recv, swap_send, swap_recv,
):
    me = lax.axis_index("blk")
    core = lax.axis_index("feat")
    other = 1 - core
    half, rows = points.shape
    feats = 2 * half
    share = rows // 2
    z = me // PLANE
    spot = me % PLANE

    def remote(src, dst, send, arrive, blk, feat):
        return pltpu.make_async_remote_copy(
            src_ref=src, dst_ref=dst, send_sem=send, recv_sem=arrive,
            device_id={"blk": blk, "feat": feat}, device_id_type=pl.DeviceIdType.MESH,
        )

    barrier = pltpu.get_barrier_semaphore()

    def greet(blk, feat):
        pl.semaphore_signal(
            barrier, inc=1, device_id={"blk": blk, "feat": feat},
            device_id_type=pl.DeviceIdType.MESH,
        )

    def plane_peer(index):
        return z * PLANE + (spot ^ index)

    def line_peer(step):
        return lax.rem(z + step, line) * PLANE + spot

    greet(me, other)
    for index in range(1, PLANE):
        greet(plane_peer(index), core)
    for step in range(1, line):
        greet(line_peer(step), core)

    my_rows = pl.ds(pl.multiple_of(core * half, half), half)
    my_vector_rows = pl.ds(pl.multiple_of(feats + core * half, half), half)

    locals_ = []
    pair = []
    for part in range(2):
        cols = pl.ds(part * share, share)
        for place, (array, spot_rows) in enumerate(((points, my_rows), (vectors, my_vector_rows))):
            slot = 2 * part + place
            target = columns.at[0, part, spot_rows, :]
            locals_.append(
                pltpu.make_async_copy(array.at[:, cols], target, local_sem.at[slot]))
            pair.append(
                remote(array.at[:, cols], target, pair_send.at[slot], pair_recv.at[slot],
                       me, other))
    locals_.append(pltpu.make_async_copy(vectors, mine, local_sem.at[4]))
    for copy in locals_:
        copy.start()
    pl.semaphore_wait(barrier, PLANE + line - 1)
    for copy in pair:
        copy.start()

    scale = outscale[0]
    top = jnp.log(jnp.full((1, 1), scale, F32)) * LOG2E
    column = jnp.transpose(jnp.broadcast_to(lengths[...], (feats, feats)))[:, 0:1]

    for copy in locals_:
        copy.wait()
    for copy in pair:
        copy.wait_recv()

    plane = []
    for index in range(1, PLANE):
        plane.append(
            remote(columns.at[0, core], columns.at[index, core], plane_send.at[index],
                   plane_recv.at[index], plane_peer(index), core))
    spread = []
    for step in range(1, line):
        spread.append(
            remote(columns.at[0, core, 0:feats, :], row_points.at[line - step],
                   row_send.at[step], row_recv.at[line - step], line_peer(step), core))
    near_first = []
    for place in range(max(len(plane), len(spread))):
        near_first += plane[place:place + 1] + spread[place:place + 1]
    for copy in near_first:
        copy.start()

    def twin(index):
        return remote(columns.at[index, core], columns.at[index, core], twin_send.at[index],
                      twin_recv.at[index], me, other)

    def other_twin(index):
        return remote(columns.at[index, other], columns.at[index, other], twin_send.at[index],
                      twin_recv.at[index], me, other)

    def fetch(index):
        plane[index - 1].wait_recv()
        twin(index).start()

    def prepare_columns(index):
        if index > 0:
            other_twin(index).wait_recv()
        for part in range(2):
            guest = (columns[index, part, 0:feats, :].astype(F32) / column).astype(BF16)
            wide = guest.astype(F32)
            norm = -0.5 * LOG2E * jnp.sum(wide * wide, axis=0, keepdims=True)
            one = jnp.ones_like(norm)
            stacked = jnp.concatenate(
                [guest, guest, guest, extra_rows(pieces(norm) + (one, one, one))], axis=0)
            right[index, part * share:(part + 1) * share, :] = stacked.T

    def prepare_rows(value):
        scaled = (value.astype(F32) / column).astype(BF16).astype(F32)
        level = -0.5 * LOG2E * jnp.sum(scaled * scaled, axis=0, keepdims=True) + top
        one = jnp.ones_like(level)
        for index, piece in enumerate(pieces(scaled * LOG2E)):
            left[index * feats:(index + 1) * feats, :] = piece.astype(BF16)
        left[3 * feats:, :] = extra_rows((one, one, one) + pieces(level))

    def unit(slot, index, start):
        power = jnp.dot(right[index], left[...], preferred_element_type=F32)
        value = jnp.exp2(jnp.minimum(power, top)).astype(BF16)
        acc = jnp.dot(columns[index, 0, feats:, :], value[0:share], preferred_element_type=F32)
        acc += jnp.dot(columns[index, 1, feats:, :], value[share:], preferred_element_type=F32)
        if start:
            total[slot] = acc
        else:
            total[slot] += acc

    def give_back(step):
        return remote(total.at[step], inbox.at[line - step], part_send.at[step],
                      part_recv.at[line - step], line_peer(step), core)

    prepare_columns(0)
    prepare_rows(columns[0, core, 0:feats, :])
    unit(0, 0, True)
    fetch(1)

    def one_row(step, carry):
        row_copy = remote(columns.at[0, core, 0:feats, :], row_points.at[step],
                          row_send.at[step], row_recv.at[step], line_peer(step), core)
        row_copy.wait_recv()
        prepare_rows(row_points[step])
        for index in range(PLANE):
            if index > 0:
                @pl.when(step == 1)
                def _():
                    if index + 1 < PLANE:
                        fetch(index + 1)
                    prepare_columns(index)

            unit(step, index, index == 0)
            if index == 0:
                @pl.when(step > 1)
                def _():
                    give_back(step - 1).start()
        return carry

    lax.fori_loop(1, line, one_row, 0)

    prepare_rows(columns[0, core, 0:feats, :])
    for index in range(1, PLANE):
        unit(0, index, False)
        if index == 1:
            give_back(line - 1).start()

    def collect(step, carry):
        give_back(line - step).wait_recv()
        total[0] += inbox[step]
        return carry

    lax.fori_loop(1, line, collect, 0)

    other_rows = pl.ds(pl.multiple_of(other * half, half), half)
    swap_out[...] = total[0, other_rows, :]
    swap = remote(swap_out, swap_in, swap_send, swap_recv, me, other)
    factor = noise[0]
    my_cols = pl.ds(pl.multiple_of(core * share, share), share)
    other_cols = pl.ds(pl.multiple_of(other * share, share), share)
    result[:, my_cols] = total[0, my_rows, :] + factor * mine[:, my_cols].astype(F32)
    swap.start()
    swap.wait_recv()
    result[:, other_cols] = swap_in[...] + factor * mine[:, other_cols].astype(F32)

    swap.wait_send()
    for copy in pair + plane + spread:
        copy.wait_send()
    for index in range(1, PLANE):
        twin(index).wait_send()

    def drain(step, carry):
        give_back(step).wait_send()
        return carry

    lax.fori_loop(1, line, drain, 0)


def per_device(blk, points, vectors, lengthscale, outscale, noise):
    assert blk % PLANE == 0 and blk > PLANE
    line = blk // PLANE
    rows, half = points.shape
    feats = 2 * half
    share = rows // 2
    vmem = pl.BlockSpec(memory_space=pltpu.VMEM)
    smem = pl.BlockSpec(memory_space=pltpu.SMEM)
    anywhere = pl.BlockSpec(memory_space=pl.ANY)
    dma = pltpu.SemaphoreType.DMA
    wide = 3 * feats + EXTRA
    out = pl.pallas_call(
        functools.partial(kernel, line),
        out_shape=jax.ShapeDtypeStruct((half, rows), F32),
        in_specs=[anywhere, anywhere, vmem, smem, smem],
        out_specs=vmem,
        scratch_shapes=[
            pltpu.VMEM((PLANE, 2, 2 * feats, share), BF16),
            pltpu.VMEM((line, feats, share), BF16),
            pltpu.VMEM((PLANE, rows, wide), BF16),
            pltpu.VMEM((wide, share), BF16),
            pltpu.VMEM((line, feats, share), F32),
            pltpu.VMEM((line, feats, share), F32),
            pltpu.VMEM((half, rows), BF16),
            pltpu.VMEM((half, share), F32),
            pltpu.VMEM((half, share), F32),
            dma((5,)),
            dma((4,)),
            dma((4,)),
            dma((PLANE,)),
            dma((PLANE,)),
            dma((PLANE,)),
            dma((PLANE,)),
            dma((line,)),
            dma((line,)),
            dma((line,)),
            dma((line,)),
            dma,
            dma,
        ],
        compiler_params=pltpu.CompilerParams(collective_id=0, has_side_effects=True),
        name="plane_line_solve",
    )(points.T, vectors.T, lengthscale.reshape(1, feats), outscale, noise)
    return out.T


def solution(mesh):
    placed = (P("blk", "feat"), P("blk", "feat"), P(), P(), P())
    return jax.shard_map(
        functools.partial(per_device, mesh.shape["blk"]),
        mesh=mesh, in_specs=placed, out_specs=P("blk", "feat"), check_vma=False,
    )
```

```python
import functools

import jax
import jax.numpy as jnp
from jax import lax
from jax.experimental import pallas as pl
from jax.experimental.pallas import tpu as pltpu
from jax.sharding import PartitionSpec as P

LOG2E = 1.4426950408889634
F32 = jnp.float32
BF16 = jnp.bfloat16
EXTRA = 16
PLANE = 4


def pieces(value):
    first = value.astype(BF16).astype(F32)
    rest = value - first
    second = rest.astype(BF16).astype(F32)
    return first, second, rest - second


def extra_rows(rows):
    shape = (EXTRA, rows[0].shape[1])
    place = lax.broadcasted_iota(jnp.int32, shape, 0)
    out = jnp.zeros(shape, F32)
    for index, row in enumerate(rows):
        out = jnp.where(place == index, row, out)
    return out.astype(BF16)


def kernel(
    line, points, vectors, lengths, outscale, noise, result,
    columns, row_points, right, left, total, inbox, mine, swap_out, swap_in,
    local_sem, pair_send, pair_recv, plane_send, plane_recv, twin_send, twin_recv,
    row_send, row_recv, part_send, part_recv, swap_send, swap_recv,
):
    me = lax.axis_index("blk")
    core = lax.axis_index("feat")
    other = 1 - core
    half, rows = points.shape
    feats = 2 * half
    share = rows // 2

    def remote(src, dst, send, arrive, blk, feat):
        return pltpu.make_async_remote_copy(
            src_ref=src, dst_ref=dst, send_sem=send, recv_sem=arrive,
            device_id={"blk": blk, "feat": feat}, device_id_type=pl.DeviceIdType.MESH,
        )

    barrier = pltpu.get_barrier_semaphore()

    def greet(blk, feat):
        pl.semaphore_signal(
            barrier, inc=1, device_id={"blk": blk, "feat": feat},
            device_id_type=pl.DeviceIdType.MESH,
        )

    def column_peer(index):
        return me ^ ((index % 2) * 2 + (index // 2) * (2 * line))

    def row_peer(step):
        return me ^ (step % 2 + (step // 2) * PLANE)

    greet(me, other)
    greet(column_peer(1), core)
    greet(column_peer(2), core)
    for step in range(1, line):
        greet(row_peer(step), core)

    my_rows = pl.ds(pl.multiple_of(core * half, half), half)
    my_vector_rows = pl.ds(pl.multiple_of(feats + core * half, half), half)

    locals_ = []
    pair = []
    for part in range(2):
        cols = pl.ds(part * share, share)
        for place, (array, spot_rows) in enumerate(((points, my_rows), (vectors, my_vector_rows))):
            slot = 2 * part + place
            target = columns.at[0, part, spot_rows, :]
            locals_.append(
                pltpu.make_async_copy(array.at[:, cols], target, local_sem.at[slot]))
            pair.append(
                remote(array.at[:, cols], target, pair_send.at[slot], pair_recv.at[slot],
                       me, other))
    locals_.append(pltpu.make_async_copy(vectors, mine, local_sem.at[4]))
    for copy in locals_:
        copy.start()
    pl.semaphore_wait(barrier, 2 + line)
    for copy in pair:
        copy.start()

    scale = outscale[0]
    top = jnp.log(jnp.full((1, 1), scale, F32)) * LOG2E
    column = jnp.transpose(jnp.broadcast_to(lengths[...], (feats, feats)))[:, 0:1]

    for copy in locals_:
        copy.wait()
    for copy in pair:
        copy.wait_recv()

    def row_copy(step):
        return remote(columns.at[0, core, 0:feats, :], row_points.at[step],
                      row_send.at[step], row_recv.at[step], row_peer(step), core)

    def column_copy(index):
        source = 0 if index < 3 else 2
        return remote(columns.at[source, core], columns.at[index, core], plane_send.at[index],
                      plane_recv.at[index], column_peer(1 if index == 3 else index), core)

    def start_row(step, carry):
        row_copy(step).start()
        return carry

    lax.fori_loop(1, line, start_row, 0)
    column_copy(1).start()
    column_copy(2).start()

    def twin(index):
        return remote(columns.at[index, core], columns.at[index, core], twin_send.at[index],
                      twin_recv.at[index], me, other)

    def other_twin(index):
        return remote(columns.at[index, other], columns.at[index, other], twin_send.at[index],
                      twin_recv.at[index], me, other)

    def fetch(index):
        column_copy(index).wait_recv()
        if index == 2:
            column_copy(3).start()
        twin(index).start()

    def prepare_columns(index):
        if index > 0:
            other_twin(index).wait_recv()
        for part in range(2):
            guest = (columns[index, part, 0:feats, :].astype(F32) / column).astype(BF16)
            wide = guest.astype(F32)
            norm = -0.5 * LOG2E * jnp.sum(wide * wide, axis=0, keepdims=True)
            one = jnp.ones_like(norm)
            stacked = jnp.concatenate(
                [guest, guest, guest, extra_rows(pieces(norm) + (one, one, one))], axis=0)
            right[index, part * share:(part + 1) * share, :] = stacked.T

    def prepare_rows(step, value):
        scaled = (value.astype(F32) / column).astype(BF16).astype(F32)
        level = -0.5 * LOG2E * jnp.sum(scaled * scaled, axis=0, keepdims=True) + top
        one = jnp.ones_like(level)
        for index, piece in enumerate(pieces(scaled * LOG2E)):
            left[step, index * feats:(index + 1) * feats, :] = piece.astype(BF16)
        left[step, 3 * feats:, :] = extra_rows((one, one, one) + pieces(level))

    def unit(step, index, parts=(0, 1)):
        guests = slice(parts[0] * share, (parts[-1] + 1) * share)
        power = jnp.dot(right[index, guests, :], left[step], preferred_element_type=F32)
        value = jnp.exp2(jnp.minimum(power, top)).astype(BF16)
        for place, part in enumerate(parts):
            total[step] += jnp.dot(
                columns[index, part, feats:, :], value[place * share:(place + 1) * share],
                preferred_element_type=F32)

    def give_back(step):
        return remote(total.at[step], inbox.at[step], part_send.at[step],
                      part_recv.at[step], row_peer(step), core)

    total[...] = jnp.zeros_like(total)
    prepare_columns(0)
    for index in range(PLANE - 1):
        if index > 0:
            prepare_columns(index)

        def one_row(step, carry):
            if index == 0:
                @pl.when(step == 0)
                def _():
                    prepare_rows(step, columns[0, core, 0:feats, :])

                @pl.when(step > 0)
                def _():
                    row_copy(step).wait_recv()
                    prepare_rows(step, row_points[step])

            @pl.when(step == line - 2)
            def _():
                fetch(index + 1)

            unit(step, index)
            return carry

        lax.fori_loop(0, line, one_row, 0)

    last = PLANE - 1
    prepare_columns(last)

    def last_row(place, carry):
        step = line - 1 - place
        unit(step, last)

        @pl.when(place > 0)
        def _():
            give_back(step + 1).start()
        return carry

    lax.fori_loop(0, line - 1, last_row, 0)
    unit(0, last, (0,))
    give_back(1).start()
    unit(0, last, (1,))

    def collect(place, carry):
        step = line - 1 - place
        give_back(step).wait_recv()
        total[0] += inbox[step]
        return carry

    lax.fori_loop(0, line - 1, collect, 0)

    other_rows = pl.ds(pl.multiple_of(other * half, half), half)
    swap_out[...] = total[0, other_rows, :]
    swap = remote(swap_out, swap_in, swap_send, swap_recv, me, other)
    factor = noise[0]
    my_cols = pl.ds(pl.multiple_of(core * share, share), share)
    other_cols = pl.ds(pl.multiple_of(other * share, share), share)
    result[:, my_cols] = total[0, my_rows, :] + factor * mine[:, my_cols].astype(F32)
    swap.start()
    swap.wait_recv()
    result[:, other_cols] = swap_in[...] + factor * mine[:, other_cols].astype(F32)

    swap.wait_send()
    for copy in pair:
        copy.wait_send()
    for index in range(1, PLANE):
        column_copy(index).wait_send()
        twin(index).wait_send()

    def drain(step, carry):
        give_back(step).wait_send()
        row_copy(step).wait_send()
        return carry

    lax.fori_loop(1, line, drain, 0)


def per_device(blk, points, vectors, lengthscale, outscale, noise):
    assert blk % (2 * PLANE) == 0 and blk & (blk - 1) == 0
    line = blk // PLANE
    rows, half = points.shape
    feats = 2 * half
    share = rows // 2
    vmem = pl.BlockSpec(memory_space=pltpu.VMEM)
    smem = pl.BlockSpec(memory_space=pltpu.SMEM)
    anywhere = pl.BlockSpec(memory_space=pl.ANY)
    dma = pltpu.SemaphoreType.DMA
    wide = 3 * feats + EXTRA
    out = pl.pallas_call(
        functools.partial(kernel, line),
        out_shape=jax.ShapeDtypeStruct((half, rows), F32),
        in_specs=[anywhere, anywhere, vmem, smem, smem],
        out_specs=vmem,
        scratch_shapes=[
            pltpu.VMEM((PLANE, 2, 2 * feats, share), BF16),
            pltpu.VMEM((line, feats, share), BF16),
            pltpu.VMEM((PLANE, rows, wide), BF16),
            pltpu.VMEM((line, wide, share), BF16),
            pltpu.VMEM((line, feats, share), F32),
            pltpu.VMEM((line, feats, share), F32),
            pltpu.VMEM((half, rows), BF16),
            pltpu.VMEM((half, share), F32),
            pltpu.VMEM((half, share), F32),
            dma((5,)),
            dma((4,)),
            dma((4,)),
            dma((PLANE,)),
            dma((PLANE,)),
            dma((PLANE,)),
            dma((PLANE,)),
            dma((line,)),
            dma((line,)),
            dma((line,)),
            dma((line,)),
            dma,
            dma,
        ],
        compiler_params=pltpu.CompilerParams(collective_id=0, has_side_effects=True),
        name="tile_solve",
    )(points.T, vectors.T, lengthscale.reshape(1, feats), outscale, noise)
    return out.T


def solution(mesh):
    placed = (P("blk", "feat"), P("blk", "feat"), P(), P(), P())
    return jax.shard_map(
        functools.partial(per_device, mesh.shape["blk"]),
        mesh=mesh, in_specs=placed, out_specs=P("blk", "feat"), check_vma=False,
    )
```

```python
import functools

import jax
import jax.numpy as jnp
from jax import lax
from jax.experimental import pallas as pl
from jax.experimental.pallas import tpu as pltpu
from jax.sharding import PartitionSpec as P

LOG2E = 1.4426950408889634
F32 = jnp.float32
BF16 = jnp.bfloat16
EXTRA = 16
PLANE = 4


def pieces(value):
    first = value.astype(BF16).astype(F32)
    rest = value - first
    second = rest.astype(BF16).astype(F32)
    return first, second, rest - second


def extra_rows(rows):
    shape = (EXTRA, rows[0].shape[1])
    place = lax.broadcasted_iota(jnp.int32, shape, 0)
    out = jnp.zeros(shape, F32)
    for index, row in enumerate(rows):
        out = jnp.where(place == index, row, out)
    return out.astype(BF16)


def kernel(
    line, points, vectors, lengths_in, outscale_in, noise_in, result,
    lengths, outscale, noise, small_sem,
    columns, row_points, right, left, total, inbox, mine, swap_out, swap_in,
    local_sem, pair_send, pair_recv, plane_send, plane_recv, twin_send, twin_recv,
    row_send, row_recv, part_send, part_recv, swap_send, swap_recv,
):
    me = lax.axis_index("blk")
    core = lax.axis_index("feat")
    other = 1 - core
    half, rows = points.shape
    feats = 2 * half
    share = rows // 2

    def remote(src, dst, send, arrive, blk, feat):
        return pltpu.make_async_remote_copy(
            src_ref=src, dst_ref=dst, send_sem=send, recv_sem=arrive,
            device_id={"blk": blk, "feat": feat}, device_id_type=pl.DeviceIdType.MESH,
        )

    small = [
        pltpu.make_async_copy(lengths_in, lengths, small_sem.at[0]),
        pltpu.make_async_copy(outscale_in, outscale, small_sem.at[1]),
        pltpu.make_async_copy(noise_in, noise, small_sem.at[2]),
    ]
    for copy in small:
        copy.start()
    barrier = pltpu.get_barrier_semaphore()

    def greet(blk, feat):
        pl.semaphore_signal(
            barrier, inc=1, device_id={"blk": blk, "feat": feat},
            device_id_type=pl.DeviceIdType.MESH,
        )

    def column_peer(index):
        return me ^ ((index % 2) * 2 + (index // 2) * (2 * line))

    def row_peer(step):
        return me ^ (step % 2 + (step // 2) * PLANE)

    greet(me, other)
    greet(column_peer(1), core)
    greet(column_peer(2), core)
    for step in range(1, line):
        greet(row_peer(step), core)

    my_rows = pl.ds(pl.multiple_of(core * half, half), half)
    my_vector_rows = pl.ds(pl.multiple_of(feats + core * half, half), half)

    locals_ = []
    pair = []
    for part in range(2):
        cols = pl.ds(part * share, share)
        for place, (array, spot_rows) in enumerate(((points, my_rows), (vectors, my_vector_rows))):
            slot = 2 * part + place
            target = columns.at[0, part, spot_rows, :]
            locals_.append(
                pltpu.make_async_copy(array.at[:, cols], target, local_sem.at[slot]))
            pair.append(
                remote(array.at[:, cols], target, pair_send.at[slot], pair_recv.at[slot],
                       me, other))
    locals_.append(pltpu.make_async_copy(vectors, mine, local_sem.at[4]))
    for copy in locals_:
        copy.start()
    pl.semaphore_wait(barrier, 2 + line)
    for copy in pair:
        copy.start()

    for copy in small:
        copy.wait()
    scale = outscale[0]
    top = jnp.log(jnp.full((1, 1), scale, F32)) * LOG2E
    column = jnp.transpose(jnp.broadcast_to(lengths[...], (feats, feats)))[:, 0:1]

    for copy in locals_:
        copy.wait()
    for copy in pair:
        copy.wait_recv()

    def row_copy(step):
        return remote(columns.at[0, core, 0:feats, :], row_points.at[step],
                      row_send.at[step], row_recv.at[step], row_peer(step), core)

    def part_of(index, owner, piece):
        return columns.at[index, owner, pl.ds(piece * feats, feats), :]

    def column_copy(index, piece):
        source = 0 if index < 3 else 2
        return remote(part_of(source, core, piece), part_of(index, core, piece),
                      plane_send.at[index, piece], plane_recv.at[index, piece],
                      column_peer(1 if index == 3 else index), core)

    def start_row(step, carry):
        row_copy(step).start()
        return carry

    lax.fori_loop(1, line, start_row, 0)
    for piece in range(2):
        column_copy(1, piece).start()
        column_copy(2, piece).start()

    def twin(index, owner, piece):
        return remote(part_of(index, owner, piece), part_of(index, owner, piece),
                      twin_send.at[index, piece], twin_recv.at[index, piece], me, other)

    def fetch(index, piece):
        column_copy(index, piece).wait_recv()
        if index == 2:
            column_copy(3, piece).start()
        twin(index, core, piece).start()

    def prepare_columns(index):
        if index > 0:
            for piece in range(2):
                twin(index, other, piece).wait_recv()
        for part in range(2):
            guest = (columns[index, part, 0:feats, :].astype(F32) / column).astype(BF16)
            wide = guest.astype(F32)
            norm = -0.5 * LOG2E * jnp.sum(wide * wide, axis=0, keepdims=True)
            one = jnp.ones_like(norm)
            stacked = jnp.concatenate(
                [guest, guest, guest, extra_rows(pieces(norm) + (one, one, one))], axis=0)
            right[index, part * share:(part + 1) * share, :] = stacked.T

    def prepare_rows(step, value):
        scaled = (value.astype(F32) / column).astype(BF16).astype(F32)
        level = -0.5 * LOG2E * jnp.sum(scaled * scaled, axis=0, keepdims=True) + top
        one = jnp.ones_like(level)
        for index, piece in enumerate(pieces(scaled * LOG2E)):
            left[step, index * feats:(index + 1) * feats, :] = piece.astype(BF16)
        left[step, 3 * feats:, :] = extra_rows((one, one, one) + pieces(level))

    def unit(step, index, parts=(0, 1)):
        guests = slice(parts[0] * share, (parts[-1] + 1) * share)
        power = jnp.dot(right[index, guests, :], left[step], preferred_element_type=F32)
        value = jnp.exp2(jnp.minimum(power, top)).astype(BF16)
        for place, part in enumerate(parts):
            total[step] += jnp.dot(
                columns[index, part, feats:, :], value[place * share:(place + 1) * share],
                preferred_element_type=F32)

    def give_back(step):
        return remote(total.at[step], inbox.at[step], part_send.at[step],
                      part_recv.at[step], row_peer(step), core)

    total[...] = jnp.zeros_like(total)
    prepare_columns(0)
    for index in range(PLANE - 1):
        if index > 0:
            prepare_columns(index)

        def one_row(step, carry):
            if index == 0:
                @pl.when(step == 0)
                def _():
                    prepare_rows(step, columns[0, core, 0:feats, :])

                @pl.when(step > 0)
                def _():
                    row_copy(step).wait_recv()
                    prepare_rows(step, row_points[step])

            @pl.when(step == line - 2)
            def _():
                if index == 0:
                    fetch(1, 0)
                fetch(index + 1, 1)

            if index < PLANE - 2:
                @pl.when(step == line - 1)
                def _():
                    fetch(index + 2, 0)

            unit(step, index)
            return carry

        lax.fori_loop(0, line, one_row, 0)

    last = PLANE - 1
    prepare_columns(last)

    def last_row(place, carry):
        step = line - 1 - place
        unit(step, last)

        @pl.when(place > 0)
        def _():
            give_back(step + 1).start()
        return carry

    lax.fori_loop(0, line - 1, last_row, 0)
    unit(0, last, (0,))
    give_back(1).start()
    unit(0, last, (1,))

    def collect(place, carry):
        step = line - 1 - place
        give_back(step).wait_recv()
        total[0] += inbox[step]
        return carry

    lax.fori_loop(0, line - 1, collect, 0)

    other_rows = pl.ds(pl.multiple_of(other * half, half), half)
    swap_out[...] = total[0, other_rows, :]
    swap = remote(swap_out, swap_in, swap_send, swap_recv, me, other)
    factor = noise[0]
    my_cols = pl.ds(pl.multiple_of(core * share, share), share)
    other_cols = pl.ds(pl.multiple_of(other * share, share), share)
    result[:, my_cols] = total[0, my_rows, :] + factor * mine[:, my_cols].astype(F32)
    swap.start()
    swap.wait_recv()
    result[:, other_cols] = swap_in[...] + factor * mine[:, other_cols].astype(F32)

    swap.wait_send()
    for copy in pair:
        copy.wait_send()
    for index in range(1, PLANE):
        for piece in range(2):
            column_copy(index, piece).wait_send()
            twin(index, core, piece).wait_send()

    def drain(step, carry):
        give_back(step).wait_send()
        row_copy(step).wait_send()
        return carry

    lax.fori_loop(1, line, drain, 0)


def per_device(blk, points, vectors, lengthscale, outscale, noise):
    assert blk % (2 * PLANE) == 0 and blk & (blk - 1) == 0
    line = blk // PLANE
    rows, half = points.shape
    feats = 2 * half
    share = rows // 2
    vmem = pl.BlockSpec(memory_space=pltpu.VMEM)
    stay = pl.BlockSpec(memory_space=pltpu.HBM)
    dma = pltpu.SemaphoreType.DMA
    wide = 3 * feats + EXTRA
    out = pl.pallas_call(
        functools.partial(kernel, line),
        out_shape=jax.ShapeDtypeStruct((half, rows), F32),
        in_specs=[stay] * 5,
        out_specs=vmem,
        scratch_shapes=[
            pltpu.VMEM((1, feats), F32),
            pltpu.SMEM((1,), F32),
            pltpu.SMEM((1,), F32),
            dma((3,)),
            pltpu.VMEM((PLANE, 2, 2 * feats, share), BF16),
            pltpu.VMEM((line, feats, share), BF16),
            pltpu.VMEM((PLANE, rows, wide), BF16),
            pltpu.VMEM((line, wide, share), BF16),
            pltpu.VMEM((line, feats, share), F32),
            pltpu.VMEM((line, feats, share), F32),
            pltpu.VMEM((half, rows), BF16),
            pltpu.VMEM((half, share), F32),
            pltpu.VMEM((half, share), F32),
            dma((5,)),
            dma((4,)),
            dma((4,)),
            dma((PLANE, 2)),
            dma((PLANE, 2)),
            dma((PLANE, 2)),
            dma((PLANE, 2)),
            dma((line,)),
            dma((line,)),
            dma((line,)),
            dma((line,)),
            dma,
            dma,
        ],
        compiler_params=pltpu.CompilerParams(collective_id=0, has_side_effects=True),
        name="tile_solve",
    )(points.T, vectors.T, lengthscale.reshape(1, feats), outscale, noise)
    return out.T


def solution(mesh):
    placed = (P("blk", "feat"), P("blk", "feat"), P(), P(), P())
    return jax.shard_map(
        functools.partial(per_device, mesh.shape["blk"]),
        mesh=mesh, in_specs=placed, out_specs=P("blk", "feat"), check_vma=False,
    )
```
